32 devices in a mesh: fsdp: 32 (over z, y, x, core).
Axes of the slice: x: 2, y: 2, z: 4, core: 2. Of those that a mesh axis runs over, the one named last changes fastest.
Arguments:
- block_in: bfloat16 [64, 101, 768], P('fsdp'), may hold values from -6 to 6
- out_grad: bfloat16 [64, 101, 768], P('fsdp'), may hold values from -6 to 6
- image_counts: int32 [32], P('fsdp'), may hold values from 1 to 2, as said below
- ln1_gain: bfloat16 [768], P('fsdp'), may hold values from 0.5 to 1.5
- ln1_bias: bfloat16 [768], P('fsdp'), may hold values from -1.75 to 1.75
- w_qkv: bfloat16 [768, 2304], P('fsdp'), may hold values from -0.21875 to 0.21875
- q_bias: bfloat16 [768], P('fsdp'), may hold values from -3 to 3
- v_bias: bfloat16 [768], P('fsdp'), may hold values from -3 to 3
- w_out: bfloat16 [768, 768], P(None, 'fsdp'), may hold values from -1.75 to 1.75
- out_bias: bfloat16 [768], P('fsdp'), may hold values from -3 to 3
- ln2_gain: bfloat16 [768], P('fsdp'), may hold values from 0.5 to 1.5
- ln2_bias: bfloat16 [768], P('fsdp'), may hold values from -1.75 to 1.75
- w_up: bfloat16 [768, 3072], P('fsdp'), may hold values from -0.21875 to 0.21875
- up_bias: bfloat16 [3072], P('fsdp'), may hold values from -3 to 3
- w_down: bfloat16 [3072, 768], P(None, 'fsdp'), may hold values from -0.109375 to 0.109375
- down_bias: bfloat16 [768], P('fsdp'), may hold values from -3 to 3
Outputs:
- block_out: bfloat16 [64, 101, 768], P('fsdp')
- in_grad: bfloat16 [64, 101, 768], P('fsdp')
- grad_ln1_gain: float32 [768], P('fsdp')
- grad_ln1_bias: float32 [768], P('fsdp')
- grad_w_qkv: float32 [768, 2304], P('fsdp')
- grad_q_bias: float32 [768], P('fsdp')
- grad_v_bias: float32 [768], P('fsdp')
- grad_w_out: float32 [768, 768], P(None, 'fsdp')
- grad_out_bias: float32 [768], P('fsdp')
- grad_ln2_gain: float32 [768], P('fsdp')
- grad_ln2_bias: float32 [768], P('fsdp')
- grad_w_up: float32 [768, 3072], P('fsdp')
- grad_up_bias: float32 [3072], P('fsdp')
- grad_w_down: float32 [3072, 768], P(None, 'fsdp')
- grad_down_bias: float32 [768], P('fsdp')
The draws below stay inside these ranges and needn't reach their ends.
Inputs may be any that keep to these rules, and one draw needn't show every extreme that they name: `image_counts`: every device holds at least one live image; some device holds 2.
All inputs are finite; a program needn't handle non-finite values.
Results may differ from the reference program's by a relative error of at most 0.014.
Values may be sent and summed in bfloat16 or wider, within the bound.
A program may use at most 192 MiB of HBM per device.

```python
import math
import jax
import jax.numpy as jnp
from jax import lax

D = 768
FF = 3072
HEAD_DIM = 64
SEQ = 101
IMG_DEV = 2
IMAGES = 64
N_FSDP = 32


def draw_image_counts(key, part):
    first_key = jax.random.fold_in(key, 11)
    second_key = jax.random.fold_in(key, 23)
    drawn = jax.random.randint(first_key, (N_FSDP,), 1, IMG_DEV + 1)
    spot_full = jax.random.randint(second_key, (), 0, N_FSDP)
    spot_single = (spot_full + 1) % N_FSDP
    drawn = drawn.at[spot_full].set(IMG_DEV)
    drawn = drawn.at[spot_single].set(1)
    return drawn.astype(jnp.int32)


def raised(array, stream_key, source, target, blocks, factor):
    owner, partner = [(jnp.arange(array.shape[axis_at]) // (array.shape[axis_at] // blocks)).reshape([-1 if axis == axis_at else 1 for axis in range(array.ndim)]) for axis_at in (source, target)]
    chosen = jax.random.permutation(stream_key, blocks)[partner]
    strong = (owner == chosen) | (owner == (partner + blocks // 2) % blocks)
    return jnp.where(strong, factor * array, array)


def level_of(rng, extent, pieces, smallest, top_value):
    def one(dim, parts):
        heights = jax.random.uniform(jax.random.fold_in(jax.random.fold_in(rng, 6), dim), (parts,), jnp.float32, smallest / len(pieces), top_value / len(pieces))
        return jnp.repeat(jnp.exp(heights), extent[dim] // parts).reshape((-1,) + (1,) * (len(extent) - dim - 1))

    level = one(*pieces[0])
    for cut in pieces[1:]:
        level = level * one(*cut)
    return level


def bell_draw(key, dims, scale, bound, cuts=(), kind=jnp.bfloat16):
    values = jax.random.normal(key, dims, jnp.float32) * scale
    if len(cuts) > 0:
        values = level_of(key, dims, cuts, -0.22, 0.18) * values
    return jnp.clip(values, min=-bound, max=bound).astype(kind)


def heavy_noise(rng, dims, scale, bound, shards, heavy, held_as=jnp.bfloat16):
    array = scale * jax.random.normal(rng, dims, jnp.float32)
    if shards:
        array = array * level_of(rng, dims, shards, -0.22, 0.18)
    return jnp.clip(raised(array, jax.random.fold_in(rng, 3), *heavy), -bound, bound).astype(held_as)


def setup_inputs(seed: int = 0) -> dict:
    keys = jax.random.split(jax.random.key(seed), 17)
    block_in = heavy_noise(keys[0], (IMAGES, SEQ, D), 1.0, 6.0, ((0, 32),), (0, 2, 32, 2.75))
    out_grad = heavy_noise(keys[1], (IMAGES, SEQ, D), 1.0, 6.0, ((0, 32),), (0, 2, 32, 2.75))
    image_counts = draw_image_counts(jax.random.fold_in(keys[16], 71), 0)
    ln1_gain = jnp.clip(1.0 + 0.1 * jax.random.normal(keys[3], (D,), jnp.float32), 0.5, 1.5).astype(jnp.bfloat16)
    ln1_bias = bell_draw(keys[4], (D,), 0.3, 1.75, ((0, 32),))
    w_qkv = bell_draw(keys[5], (D, 3 * D), D ** -0.5, 0.21875, ((0, 32),))
    q_bias = bell_draw(keys[6], (D,), 0.5, 3.0, ((0, 32),))
    v_bias = bell_draw(keys[7], (D,), 0.5, 3.0, ((0, 32),))
    w_out = bell_draw(keys[8], (D, D), (D // 64) ** -0.5, 1.75, ((1, 32),))
    out_bias = bell_draw(keys[9], (D,), 0.5, 3.0, ((0, 32),))
    ln2_gain = jnp.clip(1.0 + 0.1 * jax.random.normal(keys[10], (D,), jnp.float32), 0.5, 1.5).astype(jnp.bfloat16)
    ln2_bias = bell_draw(keys[11], (D,), 0.3, 1.75, ((0, 32),))
    w_up = bell_draw(keys[12], (D, FF), D ** -0.5, 0.21875, ((0, 32),))
    up_bias = bell_draw(keys[13], (FF,), 0.5, 3.0, ((0, 32),))
    w_down = bell_draw(keys[14], (FF, D), FF ** -0.5, 0.109375, ((1, 32),))
    down_bias = bell_draw(keys[15], (D,), 0.5, 3.0, ((0, 32),))
    return {"block_in": block_in, "out_grad": out_grad, "image_counts": image_counts, "ln1_gain": ln1_gain, "ln1_bias": ln1_bias, "w_qkv": w_qkv, "q_bias": q_bias, "v_bias": v_bias, "w_out": w_out, "out_bias": out_bias, "ln2_gain": ln2_gain, "ln2_bias": ln2_bias, "w_up": w_up, "up_bias": up_bias, "w_down": w_down, "down_bias": down_bias}


NORM_EPS = 1e-06
INV_ROOT_TWO = 0.7071067811865476
INV_ROOT_TAU = 0.3989422804014327

def mixing(form, left, right):
    return jnp.einsum(form, lax.optimization_barrier(left).astype(jnp.float32), lax.optimization_barrier(right).astype(jnp.float32))

def norm_forward(stream, gain_row, offset):
    center = stream - lax.optimization_barrier(jnp.mean(stream, axis=-1, keepdims=True))
    spread = lax.rsqrt(lax.optimization_barrier(jnp.mean(center * center, axis=-1, keepdims=True)) + NORM_EPS)
    scaled = center * spread
    return (scaled * gain_row + offset, scaled, spread)

def norm_backward(upstream, scaled, spread, gain_row):
    weighted = upstream * gain_row
    return spread * (weighted - lax.optimization_barrier(jnp.mean(weighted, axis=-1, keepdims=True)) - scaled * lax.optimization_barrier(jnp.mean(weighted * scaled, axis=-1, keepdims=True)))

def gelu_value(pre_act):
    return 0.5 * pre_act * (1.0 + lax.erf(pre_act * INV_ROOT_TWO))

def gelu_slope(pre_act):
    return 0.5 * (1.0 + lax.erf(pre_act * INV_ROOT_TWO)) + pre_act * jnp.exp(-0.5 * pre_act * pre_act) * INV_ROOT_TAU

def forward(picture, params):
    ln1_gain, ln1_bias, w_qkv, q_bias, v_bias, w_out, out_bias, ln2_gain, ln2_bias, w_up, up_bias, w_down, down_bias = params
    seq_len, model_width = picture.shape
    head_count = model_width // HEAD_DIM
    query_scale = 1.0 / math.sqrt(HEAD_DIM)
    head_shape = (seq_len, head_count, HEAD_DIM)
    residual = picture.astype(jnp.float32)
    normed_f, scaled1, spread1 = norm_forward(residual, ln1_gain.astype(jnp.float32), ln1_bias.astype(jnp.float32))
    normed1 = normed_f.astype(jnp.bfloat16)
    projected = jnp.dot(normed1, w_qkv, preferred_element_type=jnp.float32)
    queries = ((projected[:, :model_width] + q_bias.astype(jnp.float32)) * query_scale).astype(jnp.bfloat16)
    key_rows = projected[:, model_width:2 * model_width].astype(jnp.bfloat16)
    value_rows = (projected[:, 2 * model_width:] + v_bias.astype(jnp.float32)).astype(jnp.bfloat16)
    scores = mixing('qhd,khd->hqk', queries.reshape(head_shape), key_rows.reshape(head_shape))
    log_total = jax.nn.logsumexp(scores, axis=-1)
    attn_probs = jnp.exp(scores - log_total[:, :, None]).astype(jnp.bfloat16)
    attended = mixing('hqk,khd->qhd', attn_probs, value_rows.reshape(head_shape)).reshape(seq_len, model_width).astype(jnp.bfloat16)
    stream = residual + jnp.dot(attended, w_out, preferred_element_type=jnp.float32) + out_bias.astype(jnp.float32)
    normed_g, scaled2, spread2 = norm_forward(stream, ln2_gain.astype(jnp.float32), ln2_bias.astype(jnp.float32))
    normed2 = normed_g.astype(jnp.bfloat16)
    pre_act = jnp.dot(normed2, w_up, preferred_element_type=jnp.float32) + up_bias.astype(jnp.float32)
    activated = gelu_value(pre_act).astype(jnp.bfloat16)
    block_out = (stream + jnp.dot(activated, w_down, preferred_element_type=jnp.float32) + down_bias.astype(jnp.float32)).astype(jnp.bfloat16)
    stashed = (normed1, scaled1, spread1, queries, key_rows, value_rows, log_total, attended, scaled2, spread2, normed2, pre_act, activated)
    return (block_out, stashed)

def backward(out_grad, params, stashed):
    ln1_gain, ln1_bias, w_qkv, q_bias, v_bias, w_out, out_bias, ln2_gain, ln2_bias, w_up, up_bias, w_down, down_bias = params
    normed1, scaled1, spread1, queries, key_rows, value_rows, log_total, attended, scaled2, spread2, normed2, pre_act, activated = stashed
    seq_len, model_width = out_grad.shape
    head_count = model_width // HEAD_DIM
    query_scale = 1.0 / math.sqrt(HEAD_DIM)
    head_shape = (seq_len, head_count, HEAD_DIM)
    cotangent = out_grad.astype(jnp.float32)
    grad_down_bias = lax.optimization_barrier(jnp.sum(cotangent, axis=0))
    grad_w_down = jnp.dot(activated.T, out_grad, preferred_element_type=jnp.float32)
    pre_grad = jnp.dot(out_grad, w_down.T, preferred_element_type=jnp.float32) * gelu_slope(pre_act)
    pre_grad_b = pre_grad.astype(jnp.bfloat16)
    grad_up_bias = lax.optimization_barrier(jnp.sum(pre_grad, axis=0))
    grad_w_up = jnp.dot(normed2.T, pre_grad_b, preferred_element_type=jnp.float32)
    normed2_grad = jnp.dot(pre_grad_b, w_up.T, preferred_element_type=jnp.float32)
    grad_ln2_gain = lax.optimization_barrier(jnp.sum(normed2_grad * scaled2, axis=0))
    grad_ln2_bias = lax.optimization_barrier(jnp.sum(normed2_grad, axis=0))
    stream_grad = cotangent + norm_backward(normed2_grad, scaled2, spread2, ln2_gain.astype(jnp.float32))
    stream_grad_b = stream_grad.astype(jnp.bfloat16)
    grad_out_bias = lax.optimization_barrier(jnp.sum(stream_grad, axis=0))
    grad_w_out = jnp.dot(attended.T, stream_grad_b, preferred_element_type=jnp.float32)
    attended_grad = jnp.dot(stream_grad_b, w_out.T, preferred_element_type=jnp.float32).astype(jnp.bfloat16).reshape(head_shape)
    query_heads = queries.reshape(head_shape)
    key_heads = key_rows.reshape(head_shape)
    value_heads = value_rows.reshape(head_shape)
    scores = mixing('qhd,khd->hqk', query_heads, key_heads)
    attn_probs = jnp.exp(scores - log_total[:, :, None])
    prob_grad = mixing('qhd,khd->hqk', attended_grad, value_heads)
    row_delta = lax.optimization_barrier(jnp.sum(attn_probs * prob_grad, axis=-1, keepdims=True))
    score_grad = (attn_probs * (prob_grad - row_delta)).astype(jnp.bfloat16)
    value_grad = mixing('hqk,qhd->khd', attn_probs.astype(jnp.bfloat16), attended_grad).reshape(seq_len, model_width)
    query_grad = mixing('hqk,khd->qhd', score_grad, key_heads).reshape(seq_len, model_width) * query_scale
    key_grad = mixing('hqk,qhd->khd', score_grad, query_heads).reshape(seq_len, model_width)
    grad_q_bias = lax.optimization_barrier(jnp.sum(query_grad, axis=0))
    grad_v_bias = lax.optimization_barrier(jnp.sum(value_grad, axis=0))
    qkv_grad = jnp.concatenate([query_grad, key_grad, value_grad], axis=1).astype(jnp.bfloat16)
    grad_w_qkv = jnp.dot(normed1.T, qkv_grad, preferred_element_type=jnp.float32)
    normed1_grad = jnp.dot(qkv_grad, w_qkv.T, preferred_element_type=jnp.float32)
    grad_ln1_gain = lax.optimization_barrier(jnp.sum(normed1_grad * scaled1, axis=0))
    grad_ln1_bias = lax.optimization_barrier(jnp.sum(normed1_grad, axis=0))
    in_grad = (stream_grad + norm_backward(normed1_grad, scaled1, spread1, ln1_gain.astype(jnp.float32))).astype(jnp.bfloat16)
    return (in_grad, (grad_ln1_gain, grad_ln1_bias, grad_w_qkv, grad_q_bias, grad_v_bias, grad_w_out, grad_out_bias, grad_ln2_gain, grad_ln2_bias, grad_w_up, grad_up_bias, grad_w_down, grad_down_bias))

def reference(block_in, out_grad, image_counts, ln1_gain, ln1_bias, w_qkv, q_bias, v_bias, w_out, out_bias, ln2_gain, ln2_bias, w_up, up_bias, w_down, down_bias):
    params = (ln1_gain, ln1_bias, w_qkv, q_bias, v_bias, w_out, out_bias, ln2_gain, ln2_bias, w_up, up_bias, w_down, down_bias)
    slot_ids = jnp.arange(IMAGES, dtype=jnp.int32)
    live_flags = slot_ids % IMG_DEV < image_counts[slot_ids // IMG_DEV]
    zero_grads = tuple((jnp.zeros(member.shape, jnp.float32) for member in params))

    def working(operands):
        picture, cot_rows = operands
        result, stashed = forward(picture, params)
        back_rows, grad_terms = backward(cot_rows, params, stashed)
        return (result, back_rows, grad_terms)

    def skipping(operands):
        empty_rows = jnp.zeros((SEQ, D), jnp.bfloat16)
        return (empty_rows, empty_rows, tuple((jnp.zeros(member.shape, jnp.float32) for member in params)))

    def step_slot(totals, item):
        picture, cot_rows, flag = item
        result, back_rows, grad_terms = lax.cond(flag, working, skipping, (picture, cot_rows))
        totals = tuple((earlier + latest for earlier, latest in zip(totals, grad_terms)))
        return (totals, (result, back_rows))
    totals, (outputs, in_grads) = lax.scan(step_slot, zero_grads, (block_in, out_grad, live_flags))
    return (outputs, in_grads, totals[0], totals[1], totals[2], totals[3], totals[4], totals[5], totals[6], totals[7], totals[8], totals[9], totals[10], totals[11], totals[12])
```

```python
import functools
import math

import jax
import jax.numpy as jnp
from jax import lax
from jax.experimental import pallas as pl
from jax.experimental.pallas import tpu as pltpu
from jax.sharding import PartitionSpec as P

HEAD_DIM = 64


NORM_EPS = 1e-06
INV_ROOT_TWO = 0.7071067811865476
INV_ROOT_TAU = 0.3989422804014327


def mixing(form, left, right):
    return jnp.einsum(form, left, right, preferred_element_type=jnp.float32)


def against(left, right):
    return lax.dot_general(left, right, (((1,), (1,)), ((), ())), preferred_element_type=jnp.float32)


def over_rows(left, right):
    product = lax.dot_general(
        left, right, (((0,), (0,)), ((), ())), preferred_element_type=jnp.float32
    )
    return product.astype(jnp.bfloat16)


def norm_forward(stream, gain_row, offset):
    center = stream - jnp.mean(stream, axis=-1, keepdims=True)
    spread = lax.rsqrt(jnp.mean(center * center, axis=-1, keepdims=True) + NORM_EPS)
    scaled = center * spread
    return (scaled * gain_row + offset, scaled, spread)


def norm_backward(upstream, scaled, spread, gain_row):
    weighted = upstream * gain_row
    return spread * (
        weighted
        - jnp.mean(weighted, axis=-1, keepdims=True)
        - scaled * jnp.mean(weighted * scaled, axis=-1, keepdims=True)
    )


def gelu_value(pre_act):
    return 0.5 * pre_act * (1.0 + lax.erf(pre_act * INV_ROOT_TWO))


def gelu_slope(pre_act):
    return (
        0.5 * (1.0 + lax.erf(pre_act * INV_ROOT_TWO))
        + pre_act * jnp.exp(-0.5 * pre_act * pre_act) * INV_ROOT_TAU
    )


def forward(pictures, params):
    (
        ln1_gain,
        ln1_bias,
        w_qkv,
        q_bias,
        v_bias,
        w_out,
        out_bias,
        ln2_gain,
        ln2_bias,
        w_up,
        up_bias,
        w_down,
        down_bias,
    ) = params
    slots, seq_len, model_width = pictures.shape
    row_count = slots * seq_len
    head_count = model_width // HEAD_DIM
    query_scale = 1.0 / math.sqrt(HEAD_DIM)
    head_shape = (slots, seq_len, head_count, HEAD_DIM)
    residual = pictures.reshape(row_count, model_width).astype(jnp.float32)
    normed_f, scaled1, spread1 = norm_forward(
        residual, ln1_gain.astype(jnp.float32), ln1_bias.astype(jnp.float32)
    )
    normed1 = normed_f.astype(jnp.bfloat16)
    projected = jnp.dot(normed1, w_qkv, preferred_element_type=jnp.float32)
    queries = ((projected[:, :model_width] + q_bias.astype(jnp.float32)) * query_scale).astype(
        jnp.bfloat16
    )
    key_rows = projected[:, model_width : 2 * model_width].astype(jnp.bfloat16)
    value_rows = (projected[:, 2 * model_width :] + v_bias.astype(jnp.float32)).astype(jnp.bfloat16)
    scores = mixing("bqhd,bkhd->bhqk", queries.reshape(head_shape), key_rows.reshape(head_shape))
    log_total = jax.nn.logsumexp(scores, axis=-1)
    attn_probs = jnp.exp(scores - log_total[..., None]).astype(jnp.bfloat16)
    attended = (
        mixing("bhqk,bkhd->bqhd", attn_probs, value_rows.reshape(head_shape))
        .reshape(row_count, model_width)
        .astype(jnp.bfloat16)
    )
    stream = (
        residual
        + against(attended, w_out)
        + out_bias.astype(jnp.float32)
    )
    normed_g, scaled2, spread2 = norm_forward(
        stream, ln2_gain.astype(jnp.float32), ln2_bias.astype(jnp.float32)
    )
    normed2 = normed_g.astype(jnp.bfloat16)
    pre_act = jnp.dot(normed2, w_up, preferred_element_type=jnp.float32) + up_bias.astype(
        jnp.float32
    )
    activated = gelu_value(pre_act).astype(jnp.bfloat16)
    block_out = (
        stream
        + against(activated, w_down)
        + down_bias.astype(jnp.float32)
    ).astype(jnp.bfloat16)
    stashed = (
        normed1,
        scaled1,
        spread1,
        queries,
        key_rows,
        value_rows,
        log_total,
        attended,
        scaled2,
        spread2,
        normed2,
        pre_act,
        activated,
    )
    return (block_out.reshape(slots, seq_len, model_width), stashed)


def backward(out_grad, params, stashed):
    (
        ln1_gain,
        ln1_bias,
        w_qkv,
        q_bias,
        v_bias,
        w_out,
        out_bias,
        ln2_gain,
        ln2_bias,
        w_up,
        up_bias,
        w_down,
        down_bias,
    ) = params
    (
        normed1,
        scaled1,
        spread1,
        queries,
        key_rows,
        value_rows,
        log_total,
        attended,
        scaled2,
        spread2,
        normed2,
        pre_act,
        activated,
    ) = stashed
    slots, seq_len, model_width = out_grad.shape
    row_count = slots * seq_len
    head_count = model_width // HEAD_DIM
    query_scale = 1.0 / math.sqrt(HEAD_DIM)
    head_shape = (slots, seq_len, head_count, HEAD_DIM)
    grad_rows = out_grad.reshape(row_count, model_width)
    cotangent = grad_rows.astype(jnp.float32)
    grad_down_bias = jnp.sum(cotangent, axis=0)
    grad_w_down = over_rows(grad_rows, activated)
    pre_grad = jnp.dot(grad_rows, w_down, preferred_element_type=jnp.float32) * gelu_slope(
        pre_act
    )
    pre_grad_b = pre_grad.astype(jnp.bfloat16)
    grad_up_bias = jnp.sum(pre_grad, axis=0)
    grad_w_up = over_rows(normed2, pre_grad_b)
    normed2_grad = against(pre_grad_b, w_up)
    grad_ln2_gain = jnp.sum(normed2_grad * scaled2, axis=0)
    grad_ln2_bias = jnp.sum(normed2_grad, axis=0)
    stream_grad = cotangent + norm_backward(
        normed2_grad, scaled2, spread2, ln2_gain.astype(jnp.float32)
    )
    stream_grad_b = stream_grad.astype(jnp.bfloat16)
    grad_out_bias = jnp.sum(stream_grad, axis=0)
    grad_w_out = over_rows(stream_grad_b, attended)
    attended_grad = (
        jnp.dot(stream_grad_b, w_out, preferred_element_type=jnp.float32)
        .astype(jnp.bfloat16)
        .reshape(head_shape)
    )
    query_heads = queries.reshape(head_shape)
    key_heads = key_rows.reshape(head_shape)
    value_heads = value_rows.reshape(head_shape)
    scores = mixing("bqhd,bkhd->bhqk", query_heads, key_heads)
    attn_probs = jnp.exp(scores - log_total[..., None])
    prob_grad = mixing("bqhd,bkhd->bhqk", attended_grad, value_heads)
    row_delta = jnp.sum(attn_probs * prob_grad, axis=-1, keepdims=True)
    score_grad = (attn_probs * (prob_grad - row_delta)).astype(jnp.bfloat16)
    value_grad = mixing("bhqk,bqhd->bkhd", attn_probs.astype(jnp.bfloat16), attended_grad).reshape(
        row_count, model_width
    )
    query_grad = (
        mixing("bhqk,bkhd->bqhd", score_grad, key_heads).reshape(row_count, model_width)
        * query_scale
    )
    key_grad = mixing("bhqk,bqhd->bkhd", score_grad, query_heads).reshape(row_count, model_width)
    grad_q_bias = jnp.sum(query_grad, axis=0)
    grad_v_bias = jnp.sum(value_grad, axis=0)
    qkv_grad = jnp.concatenate([query_grad, key_grad, value_grad], axis=1).astype(jnp.bfloat16)
    grad_w_qkv = over_rows(normed1, qkv_grad)
    normed1_grad = against(qkv_grad, w_qkv)
    grad_ln1_gain = jnp.sum(normed1_grad * scaled1, axis=0)
    grad_ln1_bias = jnp.sum(normed1_grad, axis=0)
    in_grad = (
        stream_grad + norm_backward(normed1_grad, scaled1, spread1, ln1_gain.astype(jnp.float32))
    ).astype(jnp.bfloat16)
    return (
        in_grad.reshape(slots, seq_len, model_width),
        (
            grad_ln1_gain,
            grad_ln1_bias,
            grad_w_qkv,
            grad_q_bias,
            grad_v_bias,
            grad_w_out,
            grad_out_bias,
            grad_ln2_gain,
            grad_ln2_bias,
            grad_w_up,
            grad_up_bias,
            grad_w_down,
            grad_down_bias,
        ),
    )


def bit_orders(bit_total):
    links = list(range(bit_total - 1, 0, -1))
    if len(links) < 3:
        return [links + [0]] * 4
    high, second, last = links[:-2], links[-2], links[-1]
    return [
        high + [second, last, 0],
        high + [last, second, 0],
        [second] + high + [last, 0],
        [last] + high + [second, 0],
    ]


def flipped(position, mask, bit_total):
    for bit in range(bit_total):
        if mask >> bit & 1:
            position = position + (1 << bit) * (1 - 2 * (position // (1 << bit) % 2))
    return position


def greet(me, bit_total):
    barrier = pltpu.get_barrier_semaphore()
    for bit in range(bit_total):
        pl.semaphore_signal(
            barrier,
            inc=1,
            device_id=(flipped(me, 1 << bit, bit_total),),
            device_id_type=pl.DeviceIdType.MESH,
        )
    pl.semaphore_wait(barrier, bit_total)


def gather_kernel(bit_total, count, *refs):
    shards, wholes = refs[:count], refs[count : 2 * count]
    own_sem, send_sem, recv_sem = refs[2 * count :]
    me = lax.axis_index("fsdp")
    orders = bit_orders(bit_total)
    greet(me, bit_total)
    copies = []

    def forward_shard(number, relative, first_step):
        order = orders[number]
        absolute = flipped(me, relative, bit_total)
        for step in range(first_step, bit_total):
            bit = order[step]
            landed = relative ^ 1 << bit
            source = shards[number] if relative == 0 else wholes[number].at[absolute]
            copy = pltpu.make_async_remote_copy(
                src_ref=source,
                dst_ref=wholes[number].at[absolute],
                send_sem=send_sem.at[number, landed],
                recv_sem=recv_sem.at[number, landed],
                device_id=(flipped(me, 1 << bit, bit_total),),
                device_id_type=pl.DeviceIdType.MESH,
            )
            copy.start()
            copies.append(copy)

    for number in range(count):
        forward_shard(number, 0, 0)
    for number in range(count):
        pltpu.make_async_copy(shards[number], wholes[number].at[me], own_sem.at[number]).start()
    for turn in range(1, 1 << bit_total):
        for number in range(count):
            order = orders[number]
            relative = sum(1 << order[step] for step in range(bit_total) if turn >> step & 1)
            absolute = flipped(me, relative, bit_total)
            arrival = pltpu.make_async_remote_copy(
                src_ref=wholes[number].at[absolute],
                dst_ref=wholes[number].at[absolute],
                send_sem=send_sem.at[number, relative],
                recv_sem=recv_sem.at[number, relative],
                device_id=(flipped(me, 1, bit_total),),
                device_id_type=pl.DeviceIdType.MESH,
            )
            arrival.wait_recv()
            forward_shard(number, relative, turn.bit_length())
    for number in range(count):
        pltpu.make_async_copy(shards[number], wholes[number].at[me], own_sem.at[number]).wait()
    for copy in copies:
        copy.wait_send()


def gather_all(shards, parts):
    count, bit_total = len(shards), parts.bit_length() - 1
    return pl.pallas_call(
        functools.partial(gather_kernel, bit_total, count),
        out_shape=[jax.ShapeDtypeStruct((parts,) + s.shape, s.dtype) for s in shards],
        in_specs=[pl.BlockSpec(memory_space=pltpu.VMEM)] * count,
        out_specs=[pl.BlockSpec(memory_space=pl.ANY)] * count,
        scratch_shapes=[
            pltpu.SemaphoreType.DMA((count,)),
            pltpu.SemaphoreType.DMA((count, parts)),
            pltpu.SemaphoreType.DMA((count, parts)),
        ],
        compiler_params=pltpu.CompilerParams(collective_id=0, has_side_effects=True),
    )(*shards)


def first_step(relative, order):
    for step, bit in enumerate(order):
        if relative >> bit & 1:
            return step
    return len(order)


def column_block(width):
    for size in (768, 896, 640, 512, 384, 256, 128):
        if width % size == 0:
            return size
    return width


def scatter_kernel(bit_total, count, *refs):
    terms, totals = refs[:count], refs[count : 2 * count]
    landed = refs[2 * count : 3 * count]
    send_sem, recv_sem = refs[3 * count :]
    me = lax.axis_index("fsdp")
    orders = [order[::-1] for order in bit_orders(bit_total)]
    greet(me, bit_total)
    copies = []


    def place(number, relative, step):
        bits = [bit for bit in orders[number][step + 1 :]]
        index = sum(1 << i for i, bit in enumerate(bits) if relative >> bit & 1)
        return sum(1 << bit_total - 1 - s for s in range(step)) + index

    def summed(number, relative, steps, target):
        absolute = flipped(me, relative, bit_total)
        width = terms[number].shape[2]
        size = column_block(width)
        for step in range(steps):
            slot = place(number, relative, step)
            pltpu.make_async_remote_copy(
                src_ref=landed[number].at[slot],
                dst_ref=landed[number].at[slot],
                send_sem=send_sem.at[number, slot],
                recv_sem=recv_sem.at[number, slot],
                device_id=(flipped(me, 1, bit_total),),
                device_id_type=pl.DeviceIdType.MESH,
            ).wait_recv()

        def one(block, carry):
            columns = pl.ds(pl.multiple_of(block * size, size), size)
            total = terms[number][absolute, :, columns].astype(jnp.float32)
            for step in range(steps):
                total = total + landed[number][
                    place(number, relative, step), :, columns
                ].astype(jnp.float32)
            target[:, columns] = total.astype(target.dtype)
            return carry

        lax.fori_loop(0, width // size, one, 0)

    for step in range(bit_total):
        names = []
        for number in range(count):
            order = orders[number]
            later = [
                sum(1 << order[step + 1 + i] for i in range(bit_total - 1 - step) if turn >> i & 1)
                for turn in range(1 << bit_total - 1 - step)
            ]
            later.sort(key=lambda r: first_step(r, order))
            names.append(later)
        for turn in range(1 << bit_total - 1 - step):
            for number in range(count):
                order = orders[number]
                kept = names[number][turn]
                relative = kept | 1 << order[step]
                absolute = flipped(me, relative, bit_total)
                if step == 0:
                    source = terms[number].at[absolute]
                else:
                    source = landed[number].at[place(number, relative, 0)]
                    summed(number, relative, step, source)
                slot = place(number, kept, step)
                copy = pltpu.make_async_remote_copy(
                    src_ref=source,
                    dst_ref=landed[number].at[slot],
                    send_sem=send_sem.at[number, slot],
                    recv_sem=recv_sem.at[number, slot],
                    device_id=(flipped(me, 1 << order[step], bit_total),),
                    device_id_type=pl.DeviceIdType.MESH,
                )
                copy.start()
                copies.append(copy)
    for number in range(count):
        summed(number, 0, bit_total, totals[number])
    for copy in copies:
        copy.wait_send()


def scatter_all(terms, parts):
    count, bit_total = len(terms), parts.bit_length() - 1
    return pl.pallas_call(
        functools.partial(scatter_kernel, bit_total, count),
        out_shape=[jax.ShapeDtypeStruct(t.shape[1:], jnp.float32) for t in terms],
        in_specs=[pl.BlockSpec(memory_space=pltpu.VMEM)] * count,
        out_specs=[pl.BlockSpec(memory_space=pltpu.VMEM)] * count,
        scratch_shapes=[pltpu.VMEM((parts - 1,) + t.shape[1:], t.dtype) for t in terms]
        + [
            pltpu.SemaphoreType.DMA((count, parts)),
            pltpu.SemaphoreType.DMA((count, parts)),
        ],
        compiler_params=pltpu.CompilerParams(
            collective_id=1, has_side_effects=True, vmem_limit_bytes=60 * 1024 * 1024
        ),
    )(*terms)


def body(
    block_in,
    out_grad,
    image_counts,
    ln1_gain,
    ln1_bias,
    w_qkv,
    q_bias,
    v_bias,
    w_out,
    out_bias,
    ln2_gain,
    ln2_bias,
    w_up,
    up_bias,
    w_down,
    down_bias,
):
    parts = lax.axis_size("fsdp")
    held_count = image_counts[0]
    slot_count, _, model_width = block_in.shape
    rows = w_qkv.shape[0]
    with_kernels = rows % 8 == 0 and parts & parts - 1 == 0
    vectors = (ln1_gain, ln1_bias, q_bias, v_bias, out_bias, ln2_gain, ln2_bias, down_bias)
    small = jnp.concatenate(
        [jnp.stack(vectors, axis=1), up_bias.reshape(rows, -1)], axis=1
    )
    small_width = small.shape[1]
    padding = -small_width % 128
    small = jnp.pad(small, ((0, 0), (0, padding)))
    shards = (w_qkv, jnp.concatenate([w_out.T, small], axis=1), w_up, w_down.T)
    if with_kernels:
        wholes = gather_all(shards, parts)
    else:
        wholes = [lax.all_gather(s, "fsdp", axis=0, tiled=False) for s in shards]
    w_qkv, mixed, w_up, w_down = [w.reshape(parts * rows, w.shape[2]) for w in wholes]
    w_out = mixed[:, :model_width]
    small = mixed[:, model_width : model_width + small_width]
    ln1_gain, ln1_bias, q_bias, v_bias, out_bias, ln2_gain, ln2_bias, down_bias = small[:, :8].T
    up_bias = small[:, 8:].reshape(-1)
    gathered = (
        ln1_gain,
        ln1_bias,
        w_qkv,
        q_bias,
        v_bias,
        w_out,
        out_bias,
        ln2_gain,
        ln2_bias,
        w_up,
        up_bias,
        w_down,
        down_bias,
    )
    live_slots = (jnp.arange(slot_count, dtype=jnp.int32) < held_count)[:, None, None]
    result, stashed = forward(block_in, gathered)
    masked_grad = jnp.where(live_slots, out_grad, jnp.zeros_like(out_grad))
    back_rows, grad_terms = backward(masked_grad, gathered, stashed)
    block_out = jnp.where(live_slots, result, jnp.zeros_like(result))
    in_grad = jnp.where(live_slots, back_rows, jnp.zeros_like(back_rows))

    g_vectors = [grad_terms[i] for i in (0, 1, 3, 4, 6, 7, 8, 12)]
    g_small = jnp.concatenate(
        [jnp.stack(g_vectors, axis=1), grad_terms[10].reshape(parts * rows, -1)], axis=1
    ).astype(jnp.bfloat16)
    g_small = jnp.pad(g_small, ((0, 0), (0, padding)))
    terms = (
        grad_terms[2],
        jnp.concatenate([grad_terms[5], g_small], axis=1),
        grad_terms[9],
        grad_terms[11],
    )
    terms = [t.reshape(parts, rows, t.shape[1]) for t in terms]
    if with_kernels:
        totals = scatter_all(terms, parts)
    else:
        totals = [
            lax.psum_scatter(t.astype(jnp.float32), "fsdp", scatter_dimension=0, tiled=False)
            for t in terms
        ]
    t_qkv, t_mixed, t_up, t_down = totals
    t_out = t_mixed[:, :model_width].T
    t_small = t_mixed[:, model_width : model_width + small_width]
    t_ln1_gain, t_ln1_bias, t_q, t_v, t_out_bias, t_ln2_gain, t_ln2_bias, t_down_bias = t_small[
        :, :8
    ].T
    return (
        block_out,
        in_grad,
        t_ln1_gain,
        t_ln1_bias,
        t_qkv,
        t_q,
        t_v,
        t_out,
        t_out_bias,
        t_ln2_gain,
        t_ln2_bias,
        t_up,
        t_small[:, 8:].reshape(-1),
        t_down.T,
        t_down_bias,
    )


def solution(mesh):
    return jax.shard_map(
        body,
        mesh=mesh,
        in_specs=(
            P("fsdp", None, None),
            P("fsdp", None, None),
            P("fsdp"),
            P("fsdp"),
            P("fsdp"),
            P("fsdp", None),
            P("fsdp"),
            P("fsdp"),
            P(None, "fsdp"),
            P("fsdp"),
            P("fsdp"),
            P("fsdp"),
            P("fsdp", None),
            P("fsdp"),
            P(None, "fsdp"),
            P("fsdp"),
        ),
        out_specs=(
            P("fsdp", None, None),
            P("fsdp", None, None),
            P("fsdp"),
            P("fsdp"),
            P("fsdp", None),
            P("fsdp"),
            P("fsdp"),
            P(None, "fsdp"),
            P("fsdp"),
            P("fsdp"),
            P("fsdp"),
            P("fsdp", None),
            P("fsdp"),
            P(None, "fsdp"),
            P("fsdp"),
        ),
        check_vma=False,
    )
```

```python
import functools
import math

import jax
import jax.numpy as jnp
from jax import lax
from jax.experimental import pallas as pl
from jax.experimental.pallas import tpu as pltpu
from jax.sharding import PartitionSpec as P

HEAD_DIM = 64


NORM_EPS = 1e-06
INV_ROOT_TWO = 0.7071067811865476
INV_ROOT_TAU = 0.3989422804014327


def mixing(form, left, right):
    return jnp.einsum(form, left, right, preferred_element_type=jnp.float32)


def against(left, right):
    return lax.dot_general(left, right, (((1,), (1,)), ((), ())), preferred_element_type=jnp.float32)


def over_rows(left, right):
    product = lax.dot_general(
        left, right, (((0,), (0,)), ((), ())), preferred_element_type=jnp.float32
    )
    return product.astype(jnp.bfloat16)


def norm_forward(stream, gain_row, offset):
    center = stream - jnp.mean(stream, axis=-1, keepdims=True)
    spread = lax.rsqrt(jnp.mean(center * center, axis=-1, keepdims=True) + NORM_EPS)
    scaled = center * spread
    return (scaled * gain_row + offset, scaled, spread)


def norm_backward(upstream, scaled, spread, gain_row):
    weighted = upstream * gain_row
    return spread * (
        weighted
        - jnp.mean(weighted, axis=-1, keepdims=True)
        - scaled * jnp.mean(weighted * scaled, axis=-1, keepdims=True)
    )


def gelu_value(pre_act):
    return 0.5 * pre_act * (1.0 + lax.erf(pre_act * INV_ROOT_TWO))


def gelu_slope(pre_act):
    return (
        0.5 * (1.0 + lax.erf(pre_act * INV_ROOT_TWO))
        + pre_act * jnp.exp(-0.5 * pre_act * pre_act) * INV_ROOT_TAU
    )


def forward(pictures, params):
    (
        ln1_gain,
        ln1_bias,
        w_qkv,
        q_bias,
        v_bias,
        w_out,
        out_bias,
        ln2_gain,
        ln2_bias,
        w_up,
        up_bias,
        w_down,
        down_bias,
    ) = params
    slots, seq_len, model_width = pictures.shape
    row_count = slots * seq_len
    head_count = model_width // HEAD_DIM
    query_scale = 1.0 / math.sqrt(HEAD_DIM)
    head_shape = (slots, seq_len, head_count, HEAD_DIM)
    residual = pictures.reshape(row_count, model_width).astype(jnp.float32)
    normed_f, scaled1, spread1 = norm_forward(
        residual, ln1_gain.astype(jnp.float32), ln1_bias.astype(jnp.float32)
    )
    normed1 = normed_f.astype(jnp.bfloat16)
    projected = jnp.dot(normed1, w_qkv, preferred_element_type=jnp.float32)
    queries = ((projected[:, :model_width] + q_bias.astype(jnp.float32)) * query_scale).astype(
        jnp.bfloat16
    )
    key_rows = projected[:, model_width : 2 * model_width].astype(jnp.bfloat16)
    value_rows = (projected[:, 2 * model_width :] + v_bias.astype(jnp.float32)).astype(jnp.bfloat16)
    scores = mixing("bqhd,bkhd->bhqk", queries.reshape(head_shape), key_rows.reshape(head_shape))
    log_total = jax.nn.logsumexp(scores, axis=-1)
    attn_probs = jnp.exp(scores - log_total[..., None]).astype(jnp.bfloat16)
    attended = (
        mixing("bhqk,bkhd->bqhd", attn_probs, value_rows.reshape(head_shape))
        .reshape(row_count, model_width)
        .astype(jnp.bfloat16)
    )
    stream = (
        residual
        + against(attended, w_out)
        + out_bias.astype(jnp.float32)
    )
    normed_g, scaled2, spread2 = norm_forward(
        stream, ln2_gain.astype(jnp.float32), ln2_bias.astype(jnp.float32)
    )
    normed2 = normed_g.astype(jnp.bfloat16)
    pre_act = jnp.dot(normed2, w_up, preferred_element_type=jnp.float32) + up_bias.astype(
        jnp.float32
    )
    activated = gelu_value(pre_act).astype(jnp.bfloat16)
    block_out = (
        stream
        + against(activated, w_down)
        + down_bias.astype(jnp.float32)
    ).astype(jnp.bfloat16)
    stashed = (
        normed1,
        scaled1,
        spread1,
        queries,
        key_rows,
        value_rows,
        log_total,
        attended,
        scaled2,
        spread2,
        normed2,
        pre_act,
        activated,
    )
    return (block_out.reshape(slots, seq_len, model_width), stashed)


def backward(out_grad, params, stashed):
    (
        ln1_gain,
        ln1_bias,
        w_qkv,
        q_bias,
        v_bias,
        w_out,
        out_bias,
        ln2_gain,
        ln2_bias,
        w_up,
        up_bias,
        w_down,
        down_bias,
    ) = params
    (
        normed1,
        scaled1,
        spread1,
        queries,
        key_rows,
        value_rows,
        log_total,
        attended,
        scaled2,
        spread2,
        normed2,
        pre_act,
        activated,
    ) = stashed
    slots, seq_len, model_width = out_grad.shape
    row_count = slots * seq_len
    head_count = model_width // HEAD_DIM
    query_scale = 1.0 / math.sqrt(HEAD_DIM)
    head_shape = (slots, seq_len, head_count, HEAD_DIM)
    grad_rows = out_grad.reshape(row_count, model_width)
    cotangent = grad_rows.astype(jnp.float32)
    grad_down_bias = jnp.sum(cotangent, axis=0)
    grad_w_down = over_rows(grad_rows, activated)
    pre_grad = jnp.dot(grad_rows, w_down, preferred_element_type=jnp.float32) * gelu_slope(
        pre_act
    )
    pre_grad_b = pre_grad.astype(jnp.bfloat16)
    grad_up_bias = jnp.sum(pre_grad, axis=0)
    grad_w_up = over_rows(normed2, pre_grad_b)
    normed2_grad = against(pre_grad_b, w_up)
    grad_ln2_gain = jnp.sum(normed2_grad * scaled2, axis=0)
    grad_ln2_bias = jnp.sum(normed2_grad, axis=0)
    stream_grad = cotangent + norm_backward(
        normed2_grad, scaled2, spread2, ln2_gain.astype(jnp.float32)
    )
    stream_grad_b = stream_grad.astype(jnp.bfloat16)
    grad_out_bias = jnp.sum(stream_grad, axis=0)
    grad_w_out = over_rows(stream_grad_b, attended)
    attended_grad = (
        jnp.dot(stream_grad_b, w_out, preferred_element_type=jnp.float32)
        .astype(jnp.bfloat16)
        .reshape(head_shape)
    )
    query_heads = queries.reshape(head_shape)
    key_heads = key_rows.reshape(head_shape)
    value_heads = value_rows.reshape(head_shape)
    scores = mixing("bqhd,bkhd->bhqk", query_heads, key_heads)
    attn_probs = jnp.exp(scores - log_total[..., None])
    prob_grad = mixing("bqhd,bkhd->bhqk", attended_grad, value_heads)
    row_delta = jnp.sum(attn_probs * prob_grad, axis=-1, keepdims=True)
    score_grad = (attn_probs * (prob_grad - row_delta)).astype(jnp.bfloat16)
    value_grad = mixing("bhqk,bqhd->bkhd", attn_probs.astype(jnp.bfloat16), attended_grad).reshape(
        row_count, model_width
    )
    query_grad = (
        mixing("bhqk,bkhd->bqhd", score_grad, key_heads).reshape(row_count, model_width)
        * query_scale
    )
    key_grad = mixing("bhqk,bqhd->bkhd", score_grad, query_heads).reshape(row_count, model_width)
    grad_q_bias = jnp.sum(query_grad, axis=0)
    grad_v_bias = jnp.sum(value_grad, axis=0)
    qkv_grad = jnp.concatenate([query_grad, key_grad, value_grad], axis=1).astype(jnp.bfloat16)
    grad_w_qkv = over_rows(normed1, qkv_grad)
    normed1_grad = against(qkv_grad, w_qkv)
    grad_ln1_gain = jnp.sum(normed1_grad * scaled1, axis=0)
    grad_ln1_bias = jnp.sum(normed1_grad, axis=0)
    in_grad = (
        stream_grad + norm_backward(normed1_grad, scaled1, spread1, ln1_gain.astype(jnp.float32))
    ).astype(jnp.bfloat16)
    return (
        in_grad.reshape(slots, seq_len, model_width),
        (
            grad_ln1_gain,
            grad_ln1_bias,
            grad_w_qkv,
            grad_q_bias,
            grad_v_bias,
            grad_w_out,
            grad_out_bias,
            grad_ln2_gain,
            grad_ln2_bias,
            grad_w_up,
            grad_up_bias,
            grad_w_down,
            grad_down_bias,
        ),
    )


def bit_orders(bit_total):
    links = list(range(bit_total - 1, 0, -1))
    if len(links) < 3:
        return [links + [0]] * 4
    high, second, last = links[:-2], links[-2], links[-1]
    return [
        high + [second, last, 0],
        high + [last, second, 0],
        [second] + high + [last, 0],
        [last] + high + [second, 0],
    ]


def flipped(position, mask, bit_total):
    for bit in range(bit_total):
        if mask >> bit & 1:
            position = position + (1 << bit) * (1 - 2 * (position // (1 << bit) % 2))
    return position


def greet(me, bit_total):
    barrier = pltpu.get_barrier_semaphore()
    for bit in range(bit_total):
        pl.semaphore_signal(
            barrier,
            inc=1,
            device_id=(flipped(me, 1 << bit, bit_total),),
            device_id_type=pl.DeviceIdType.MESH,
        )
    pl.semaphore_wait(barrier, bit_total)


def gather_kernel(bit_total, count, *refs):
    shards, wholes = refs[:count], refs[count : 2 * count]
    own_sem, send_sem, recv_sem = refs[2 * count :]
    me = lax.axis_index("fsdp")
    orders = bit_orders(bit_total)
    greet(me, bit_total)
    copies = []

    def forward_shard(number, relative, first_step):
        order = orders[number]
        absolute = flipped(me, relative, bit_total)
        for step in range(first_step, bit_total):
            bit = order[step]
            landed = relative ^ 1 << bit
            source = shards[number] if relative == 0 else wholes[number].at[absolute]
            copy = pltpu.make_async_remote_copy(
                src_ref=source,
                dst_ref=wholes[number].at[absolute],
                send_sem=send_sem.at[number, landed],
                recv_sem=recv_sem.at[number, landed],
                device_id=(flipped(me, 1 << bit, bit_total),),
                device_id_type=pl.DeviceIdType.MESH,
            )
            copy.start()
            copies.append(copy)

    for number in range(count):
        forward_shard(number, 0, 0)
    for number in range(count):
        pltpu.make_async_copy(shards[number], wholes[number].at[me], own_sem.at[number]).start()
    for turn in range(1, 1 << bit_total):
        for number in range(count):
            order = orders[number]
            relative = sum(1 << order[step] for step in range(bit_total) if turn >> step & 1)
            absolute = flipped(me, relative, bit_total)
            arrival = pltpu.make_async_remote_copy(
                src_ref=wholes[number].at[absolute],
                dst_ref=wholes[number].at[absolute],
                send_sem=send_sem.at[number, relative],
                recv_sem=recv_sem.at[number, relative],
                device_id=(flipped(me, 1, bit_total),),
                device_id_type=pl.DeviceIdType.MESH,
            )
            arrival.wait_recv()
            forward_shard(number, relative, turn.bit_length())
    for number in range(count):
        pltpu.make_async_copy(shards[number], wholes[number].at[me], own_sem.at[number]).wait()
    for copy in copies:
        copy.wait_send()


def gather_all(shards, parts):
    count, bit_total = len(shards), parts.bit_length() - 1
    return pl.pallas_call(
        functools.partial(gather_kernel, bit_total, count),
        out_shape=[jax.ShapeDtypeStruct((parts,) + s.shape, s.dtype) for s in shards],
        in_specs=[pl.BlockSpec(memory_space=pltpu.VMEM)] * count,
        out_specs=[pl.BlockSpec(memory_space=pl.ANY)] * count,
        scratch_shapes=[
            pltpu.SemaphoreType.DMA((count,)),
            pltpu.SemaphoreType.DMA((count, parts)),
            pltpu.SemaphoreType.DMA((count, parts)),
        ],
        compiler_params=pltpu.CompilerParams(collective_id=0, has_side_effects=True),
    )(*shards)


def first_step(relative, order):
    for step, bit in enumerate(order):
        if relative >> bit & 1:
            return step
    return len(order)


def column_block(width):
    for size in (768, 896, 640, 512, 384, 256, 128):
        if width % size == 0:
            return size
    return width


def scatter_kernel(bit_total, count, *refs):
    terms, totals = refs[:count], refs[count : 2 * count]
    landed, held = refs[2 * count : 3 * count], refs[3 * count : 4 * count]
    send_sem, recv_sem, load_sem = refs[4 * count :]
    me = lax.axis_index("fsdp")
    orders = [order[::-1] for order in bit_orders(bit_total)]
    greet(me, bit_total)
    copies = []


    def load(number, relative):
        absolute = flipped(me, relative, bit_total)
        return pltpu.make_async_copy(
            terms[number].at[absolute],
            held[number].at[relative // 2],
            load_sem.at[number, relative // 2],
        )

    def place(number, relative, step):
        bits = [bit for bit in orders[number][step + 1 :]]
        index = sum(1 << i for i, bit in enumerate(bits) if relative >> bit & 1)
        return sum(1 << bit_total - 1 - s for s in range(step)) + index

    def summed(number, relative, steps, target):
        width = terms[number].shape[2]
        load(number, relative).wait()
        size = column_block(width)
        for step in range(steps):
            slot = place(number, relative, step)
            pltpu.make_async_remote_copy(
                src_ref=landed[number].at[slot],
                dst_ref=landed[number].at[slot],
                send_sem=send_sem.at[number, slot],
                recv_sem=recv_sem.at[number, slot],
                device_id=(flipped(me, 1, bit_total),),
                device_id_type=pl.DeviceIdType.MESH,
            ).wait_recv()

        def one(block, carry):
            columns = pl.ds(pl.multiple_of(block * size, size), size)
            total = held[number][relative // 2, :, columns].astype(jnp.float32)
            for step in range(steps):
                total = total + landed[number][
                    place(number, relative, step), :, columns
                ].astype(jnp.float32)
            target[:, columns] = total.astype(target.dtype)
            return carry

        lax.fori_loop(0, width // size, one, 0)

    for step in range(bit_total):
        names = []
        for number in range(count):
            order = orders[number]
            later = [
                sum(1 << order[step + 1 + i] for i in range(bit_total - 1 - step) if turn >> i & 1)
                for turn in range(1 << bit_total - 1 - step)
            ]
            later.sort(key=lambda r: first_step(r, order))
            names.append(later)
        for turn in range(1 << bit_total - 1 - step):
            for number in range(count):
                order = orders[number]
                kept = names[number][turn]
                relative = kept | 1 << order[step]
                absolute = flipped(me, relative, bit_total)
                if step == 0:
                    source = terms[number].at[absolute]
                else:
                    source = landed[number].at[place(number, relative, 0)]
                    summed(number, relative, step, source)
                slot = place(number, kept, step)
                copy = pltpu.make_async_remote_copy(
                    src_ref=source,
                    dst_ref=landed[number].at[slot],
                    send_sem=send_sem.at[number, slot],
                    recv_sem=recv_sem.at[number, slot],
                    device_id=(flipped(me, 1 << order[step], bit_total),),
                    device_id_type=pl.DeviceIdType.MESH,
                )
                copy.start()
                copies.append(copy)
        if step == 0:
            for turn in range(1 << bit_total - 1):
                for number in range(count):
                    load(number, names[number][turn]).start()
    for number in range(count):
        summed(number, 0, bit_total, totals[number])
    for copy in copies:
        copy.wait_send()


def scatter_all(terms, parts):
    count, bit_total = len(terms), parts.bit_length() - 1
    return pl.pallas_call(
        functools.partial(scatter_kernel, bit_total, count),
        out_shape=[jax.ShapeDtypeStruct(t.shape[1:], jnp.float32) for t in terms],
        in_specs=[pl.BlockSpec(memory_space=pl.ANY)] * count,
        out_specs=[pl.BlockSpec(memory_space=pltpu.VMEM)] * count,
        scratch_shapes=[pltpu.VMEM((parts - 1,) + t.shape[1:], t.dtype) for t in terms]
        + [pltpu.VMEM((parts // 2,) + t.shape[1:], t.dtype) for t in terms]
        + [
            pltpu.SemaphoreType.DMA((count, parts)),
            pltpu.SemaphoreType.DMA((count, parts)),
            pltpu.SemaphoreType.DMA((count, parts)),
        ],
        compiler_params=pltpu.CompilerParams(
            collective_id=1, has_side_effects=True, vmem_limit_bytes=60 * 1024 * 1024
        ),
    )(*terms)


def body(
    block_in,
    out_grad,
    image_counts,
    ln1_gain,
    ln1_bias,
    w_qkv,
    q_bias,
    v_bias,
    w_out,
    out_bias,
    ln2_gain,
    ln2_bias,
    w_up,
    up_bias,
    w_down,
    down_bias,
):
    parts = lax.axis_size("fsdp")
    held_count = image_counts[0]
    slot_count, _, model_width = block_in.shape
    rows = w_qkv.shape[0]
    with_kernels = rows % 8 == 0 and parts & parts - 1 == 0
    vectors = (ln1_gain, ln1_bias, q_bias, v_bias, out_bias, ln2_gain, ln2_bias, down_bias)
    small = jnp.concatenate(vectors + (up_bias,)).reshape(rows, -1)
    small_width = small.shape[1]
    padding = -small_width % 128
    small = jnp.pad(small, ((0, 0), (0, padding)))
    shards = (w_qkv, jnp.concatenate([w_out.T, small], axis=1), w_up, w_down.T)
    if with_kernels:
        wholes = gather_all(shards, parts)
    else:
        wholes = [lax.all_gather(s, "fsdp", axis=0, tiled=False) for s in shards]
    w_qkv, mixed, w_up, w_down = [w.reshape(parts * rows, w.shape[2]) for w in wholes]
    w_out = mixed[:, :model_width]
    small = mixed[:, model_width : model_width + small_width].reshape(parts, -1)
    ln1_gain, ln1_bias, q_bias, v_bias, out_bias, ln2_gain, ln2_bias, down_bias = [
        small[:, i * rows : (i + 1) * rows].reshape(-1) for i in range(8)
    ]
    up_bias = small[:, 8 * rows :].reshape(-1)
    gathered = (
        ln1_gain,
        ln1_bias,
        w_qkv,
        q_bias,
        v_bias,
        w_out,
        out_bias,
        ln2_gain,
        ln2_bias,
        w_up,
        up_bias,
        w_down,
        down_bias,
    )
    live_slots = (jnp.arange(slot_count, dtype=jnp.int32) < held_count)[:, None, None]
    result, stashed = forward(block_in, gathered)
    masked_grad = jnp.where(live_slots, out_grad, jnp.zeros_like(out_grad))
    back_rows, grad_terms = backward(masked_grad, gathered, stashed)
    block_out = jnp.where(live_slots, result, jnp.zeros_like(result))
    in_grad = jnp.where(live_slots, back_rows, jnp.zeros_like(back_rows))

    g_vectors = [grad_terms[i] for i in (0, 1, 3, 4, 6, 7, 8, 12)]
    g_small = jnp.concatenate(
        [g.astype(jnp.bfloat16).reshape(parts, -1) for g in g_vectors + [grad_terms[10]]], axis=1
    ).reshape(parts * rows, -1)
    g_small = jnp.pad(g_small, ((0, 0), (0, padding)))
    terms = (
        grad_terms[2],
        jnp.concatenate([grad_terms[5], g_small], axis=1),
        grad_terms[9],
        grad_terms[11],
    )
    terms = [t.reshape(parts, rows, t.shape[1]) for t in terms]
    if with_kernels:
        totals = scatter_all(terms, parts)
    else:
        totals = [
            lax.psum_scatter(t.astype(jnp.float32), "fsdp", scatter_dimension=0, tiled=False)
            for t in terms
        ]
    t_qkv, t_mixed, t_up, t_down = totals
    t_out = t_mixed[:, :model_width].T
    t_small = t_mixed[:, model_width : model_width + small_width].reshape(-1)
    t_ln1_gain, t_ln1_bias, t_q, t_v, t_out_bias, t_ln2_gain, t_ln2_bias, t_down_bias = [
        t_small[i * rows : (i + 1) * rows] for i in range(8)
    ]
    return (
        block_out,
        in_grad,
        t_ln1_gain,
        t_ln1_bias,
        t_qkv,
        t_q,
        t_v,
        t_out,
        t_out_bias,
        t_ln2_gain,
        t_ln2_bias,
        t_up,
        t_small[8 * rows :],
        t_down.T,
        t_down_bias,
    )


def solution(mesh):
    return jax.shard_map(
        body,
        mesh=mesh,
        in_specs=(
            P("fsdp", None, None),
            P("fsdp", None, None),
            P("fsdp"),
            P("fsdp"),
            P("fsdp"),
            P("fsdp", None),
            P("fsdp"),
            P("fsdp"),
            P(None, "fsdp"),
            P("fsdp"),
            P("fsdp"),
            P("fsdp"),
            P("fsdp", None),
            P("fsdp"),
            P(None, "fsdp"),
            P("fsdp"),
        ),
        out_specs=(
            P("fsdp", None, None),
            P("fsdp", None, None),
            P("fsdp"),
            P("fsdp"),
            P("fsdp", None),
            P("fsdp"),
            P("fsdp"),
            P(None, "fsdp"),
            P("fsdp"),
            P("fsdp"),
            P("fsdp"),
            P("fsdp", None),
            P("fsdp"),
            P(None, "fsdp"),
            P("fsdp"),
        ),
        check_vma=False,
    )
```
